128 devices in a mesh: dom: 16 (over z, x), band: 8 (over y, core).
Axes of the slice: x: 4, y: 4, z: 4, core: 2. Of those that a mesh axis runs over, the one named last changes fastest.
Arguments:
- orbitals_now: bfloat16 [256, 512, 512], P('dom', 'band'), may hold values from -6 to 6
- orbitals_prev: bfloat16 [256, 512, 512], P('dom', 'band'), may hold values from -6 to 6
- interp: bfloat16 [8, 512, 512], replicated, may hold values from -0.25 to 0.25
- owner_map: int32 [256], replicated, may hold values from 0 to 15, as said below
- child_oct: int32 [256, 2], replicated, may hold values from 0 to 7, all different within a row
Outputs:
- predicted: bfloat16 [1024, 512, 512], P(('dom', 'band'))
The draws below stay inside these ranges and needn't reach their ends.
Inputs may be any that keep to these rules, and one draw needn't show every extreme that they name: `owner_map`: among the 16 cells of one domain at most 2 have the same owner; in every draw one owner receives exactly 2 cells from every domain.
All inputs are finite; a program needn't handle non-finite values.
Results may differ from the reference program's by a relative error of at most 0.0059.
Values may be sent and summed in bfloat16 or wider, within the bound.
No kernel may reach another device: no remote copies, remote signals or barrier semaphores. Data moves between devices by JAX's collectives and lax.ppermute only.
A program may use at most 128 MiB of HBM per device.

```python
import math
import jax
import jax.numpy as jnp
from jax import lax

STATES = 512
NODES = 512
OCTANTS = 8
OLD_DEV = 16
CAP = 2
NEWC_DEV = 64
OLD_CELLS = 256
NEW_CELLS = 1024
N_DOM = 16


def draw_owner_map(key, part):
    key_busiest = jax.random.fold_in(key, 11)
    key_ordering = jax.random.fold_in(key, 12)
    key_offset = jax.random.fold_in(key, 13)
    busiest = jax.random.randint(key_busiest, (), 0, N_DOM)
    scores = jax.random.randint(key_ordering, (N_DOM, OLD_DEV), 0, 1 << 20) * OLD_DEV + jnp.arange(OLD_DEV, dtype=jnp.int32)[None, :]
    ordering = jnp.argsort(scores, axis=1)
    cell_ranks = jnp.argsort(ordering, axis=1).astype(jnp.int32)
    offset = jax.random.randint(key_offset, (N_DOM, 1), 0, N_DOM - 1)
    others = (cell_ranks - CAP + offset) % (N_DOM - 1)
    others = others + (others >= busiest).astype(jnp.int32)
    owners = jnp.where(cell_ranks < CAP, busiest, others)
    return owners.reshape(-1).astype(jnp.int32)


def block_levels(stream_key, extent, split, low, high):
    loudness = 1.0
    for axis_at, shards_of in split:
        heights = jax.random.uniform(jax.random.fold_in(jax.random.fold_in(stream_key, 6), axis_at), (shards_of,), jnp.float32, low / len(split), high / len(split))
        loudness = loudness * jnp.repeat(jnp.exp(heights), extent[axis_at] // shards_of).reshape((-1,) + (1,) * (len(extent) - 1 - axis_at))
    return loudness


def choose_distinct(rng, rows, number_of, top, lift):
    ranking = jax.random.permutation(jax.random.fold_in(rng, 1), number_of)
    boost = ranking
    for power in range(3):
        boost = boost * boost // number_of
    boost = boost * lift // number_of
    chance = jax.random.randint(jax.random.fold_in(rng, 2), (rows, number_of), 0, 4096) + boost
    holders = jax.random.permutation(jax.random.fold_in(rng, 3), rows)[jnp.arange(number_of) % rows]
    chance = jnp.where(jnp.arange(rows)[:, None] == holders[None, :], 1 << 14, chance)
    priority = chance * number_of + jnp.arange(number_of)
    return lax.top_k(priority.astype(jnp.int32), top)[1].astype(jnp.int32)


def normal_values(stream_key, extent, deviation, reach, pieces=(), kind=jnp.bfloat16):
    loudness = block_levels(stream_key, extent, pieces, -0.22, 0.18) if pieces else 1.0
    values = jax.random.normal(stream_key, extent, jnp.float32) * deviation * loudness
    return jnp.minimum(jnp.maximum(values, -reach), reach).astype(kind)


def setup_inputs(seed: int = 0) -> dict:
    splits = jax.random.split(jax.random.key(seed), 6)
    orbitals_now = normal_values(splits[0], (OLD_CELLS, STATES, NODES), 1.0, 6.0, ((0, 16), (1, 8)))
    orbitals_prev = normal_values(splits[1], (OLD_CELLS, STATES, NODES), 1.0, 6.0, ((0, 16), (1, 8)))
    interp = normal_values(splits[2], (OCTANTS, NODES, NODES), NODES ** -0.5, 0.25)
    owner_map = draw_owner_map(jax.random.fold_in(splits[5], 71), 0)
    child_oct = choose_distinct(splits[4], OLD_CELLS, OCTANTS, 2, 0)
    return dict(orbitals_now=orbitals_now, orbitals_prev=orbitals_prev, interp=interp, owner_map=owner_map, child_oct=child_oct)


def ranks_of(owners):
    matching = owners[:, :, None] == owners[:, None, :]
    positions = jnp.arange(OLD_DEV, dtype=jnp.int32)
    earlier = positions[None, :] < positions[:, None]
    return lax.optimization_barrier(jnp.sum((matching & earlier[None]).astype(jnp.int32), axis=2)).astype(jnp.int32)

def refine(stacked, octants, interp):

    def refine_cell(inputs):
        parent, picked = inputs
        matrices = interp[picked].astype(jnp.float32)
        return jnp.einsum('sn,jmn->jsm', parent.astype(jnp.float32), matrices).astype(jnp.bfloat16)
    return lax.map(refine_cell, (stacked, octants))

def reference(orbitals_now, orbitals_prev, interp, owner_map, child_oct):
    owners = owner_map.reshape(N_DOM, OLD_DEV).astype(jnp.int32)
    cell_ranks = ranks_of(owners)
    sources = jnp.arange(N_DOM, dtype=jnp.int32)[:, None]
    parent_slot = (owners * NEWC_DEV + (sources * CAP + cell_ranks) * 2).astype(jnp.int32)
    new_index = (parent_slot.reshape(-1, 1) + jnp.arange(2, dtype=jnp.int32)[None, :]).reshape(-1).astype(jnp.int32)
    stacked = jnp.concatenate([orbitals_now, orbitals_prev], axis=1)
    children = refine(stacked, child_oct.astype(jnp.int32), interp)
    cells = children.reshape(-1, 2 * STATES, NODES)

    def accumulate(total, cell):
        return (total + jnp.dot(cell[:STATES], cell[STATES:].T, preferred_element_type=jnp.float32), None)
    zeros_st = jnp.zeros((STATES, STATES), jnp.float32)
    total, _ = lax.scan(accumulate, zeros_st, cells)
    scaling = 1.0 / math.sqrt(2.0 * STATES * OLD_CELLS * NODES)
    intersection_b = (total * scaling).astype(jnp.bfloat16)

    def predict_cell(cell):
        mixed = jnp.dot(intersection_b.T, cell[:STATES], preferred_element_type=jnp.float32)
        return (cell[STATES:].astype(jnp.float32) + mixed).astype(jnp.bfloat16)
    values = lax.map(predict_cell, cells)
    return jnp.zeros((NEW_CELLS, STATES, NODES), jnp.bfloat16).at[new_index].set(values)
```

```python
import functools
import math

import jax
import jax.numpy as jnp
from jax import lax
from jax.experimental import pallas as pl
from jax.experimental.pallas import tpu as pltpu
from jax.sharding import Mesh
from jax.sharding import PartitionSpec as P

Z, X, Y, C = "dom_0", "dom_1", "band_0", "band_1"
DOM = (Z, X)
BAND = (Y, C)
DOM_BAND = (Z, X, Y, C)
CHIPS = (Z, X, Y)

BF16 = jnp.bfloat16
F32 = jnp.float32
RING = 4
CORES = 2
OFFSETS = tuple((q, l) for q in range(RING) for l in range(CORES))


SMEM = pl.BlockSpec(memory_space=pltpu.SMEM)
ANY = pl.BlockSpec(memory_space=pl.ANY)


def ring_pairs(shift):
    return [(i, (i + shift) % RING) for i in range(RING)]


def band_pairs(q, l):
    return [
        (y * CORES + c, ((y + q) % RING) * CORES + (c + l) % CORES)
        for y in range(RING)
        for c in range(CORES)
    ]


def round_ring(pieces, axis):
    return [pieces[0]] + [
        lax.ppermute(pieces[k], axis, ring_pairs(k)) for k in range(1, RING)
    ]


def over_band(pieces):
    return [
        piece if (q, l) == (0, 0) else lax.ppermute(piece, BAND, band_pairs(q, l))
        for (q, l), piece in zip(OFFSETS, pieces)
    ]


def run_copies(copies):
    for copy in copies:
        copy.start()
    for copy in copies:
        copy.wait()


def sized(shape, dtype=BF16):
    return jax.ShapeDtypeStruct(shape, dtype)


def moved(read, written, flops=0):
    return pl.CostEstimate(flops=flops, bytes_accessed=read + written, transcendentals=0)


def cells_kernel(at, now, prev, *refs):
    outs, (buf, in_sem, out_sem) = refs[:7], refs[7:]
    y, c = at[2], at[3]
    loads, stores = [], []
    for n, (q, l) in enumerate(OFFSETS[1:]):
        first = (((y + q) & 3) * CORES + ((c + l) & 1)) * 2
        loads.append(
            [
                pltpu.make_async_copy(src.at[pl.ds(first, 2)], buf.at[n, a], in_sem.at[n, a])
                for a, src in enumerate((now, prev))
            ]
        )
        stores.append(pltpu.make_async_copy(buf.at[n], outs[n], out_sem.at[n]))
    for pair in loads:
        for copy in pair:
            copy.start()
    for pair, store in zip(loads, stores):
        for copy in pair:
            copy.wait()
        store.start()
    for store in stores:
        store.wait()


def cells_for_band(at, now, prev):
    _, rows, nodes = now.shape
    piece = (2, 2, rows, nodes)
    size = 4 * rows * nodes * 2
    return pl.pallas_call(
        cells_kernel,
        out_shape=[sized(piece)] * 7,
        in_specs=[SMEM, ANY, ANY],
        out_specs=[ANY] * 7,
        scratch_shapes=[
            pltpu.VMEM((7, *piece), BF16),
            pltpu.SemaphoreType.DMA((7, 2)),
            pltpu.SemaphoreType.DMA((7,)),
        ],
        cost_estimate=moved(7 * size, 7 * size),
        name="cells_for_band",
    )(at, now, prev)


def product_kernel(at, octants, now, prev, *refs):
    pieces, interp, mine, other = refs[:7], refs[7], refs[8], refs[9]
    parents, matrices, kids, out, in_sem, mat_sem, out_sem = refs[10:]
    z, x, y, c = at[0], at[1], at[2], at[3]
    rows = now.shape[1]
    nodes = now.shape[2]
    states = parents.shape[2]
    half = states // 2
    first = (y * CORES + c) * 2
    cell0 = (z * RING + x) * now.shape[0] + first
    copies = []
    for e in range(2):
        for j in range(2):
            o = octants[(cell0 + e) * 2 + j]
            copies.append(
                pltpu.make_async_copy(interp.at[o], matrices.at[e, j], mat_sem.at[e, j])
            )
    own = pl.ds(pl.multiple_of((y * CORES + c) * rows, rows), rows)
    for a, src in enumerate((now, prev)):
        copies.append(
            pltpu.make_async_copy(
                src.at[pl.ds(first, 2)], parents.at[a, :, own], in_sem.at[7 + a]
            )
        )
    for n, (q, l) in enumerate(OFFSETS[1:]):
        b = ((y - q) & 3) * CORES + ((c - l) & 1)
        to = pl.ds(pl.multiple_of(b * rows, rows), rows)
        copies.append(
            pltpu.make_async_copy(pieces[n], parents.at[:, :, to], in_sem.at[n])
        )
    run_copies(copies)
    for a in range(2):
        for e in range(2):
            for j in range(2):
                kids[a, :, pl.ds((e * 2 + j) * nodes, nodes)] = lax.dot_general(
                    parents[a, e],
                    matrices[e, j],
                    (((1,), (1,)), ((), ())),
                    preferred_element_type=F32,
                ).astype(BF16)
    stores = []
    for n, (side, dst) in enumerate(((c, mine), (1 - c, other))):
        u = pl.ds(pl.multiple_of(side * half, half), half)
        part = lax.dot_general(
            kids[1, u, :], kids[0], (((1,), (1,)), ((), ())), preferred_element_type=F32
        )
        for t in range(states // 128):
            out[n, t] = part[:, t * 128 : (t + 1) * 128]
        stores.append(pltpu.make_async_copy(out.at[n], dst, out_sem.at[n]))
        stores[-1].start()
    for store in stores:
        store.wait()


def product_of_cells(at, octants, now, prev, pieces, interp):
    _, rows, nodes = now.shape
    states = rows * RING * CORES
    lanes = (states // 128, states // 2, 128)
    return pl.pallas_call(
        product_kernel,
        out_shape=[sized(lanes, F32)] * 2,
        in_specs=[SMEM, SMEM] + [ANY] * 10,
        out_specs=[ANY] * 2,
        scratch_shapes=[
            pltpu.VMEM((2, 2, states, nodes), BF16),
            pltpu.VMEM((2, 2, nodes, nodes), BF16),
            pltpu.VMEM((2, states, 4 * nodes), BF16),
            pltpu.VMEM((2, *lanes), F32),
            pltpu.SemaphoreType.DMA((9,)),
            pltpu.SemaphoreType.DMA((2, 2)),
            pltpu.SemaphoreType.DMA((2,)),
        ],
        cost_estimate=moved(4 << 20, 1 << 20, 24 * states * nodes * nodes),
        name="product_of_cells",
    )(at, octants, now, prev, *pieces, interp)


def summed_over_all(mine, other, scaling):
    swap = [(0, 1), (1, 0)]
    half = mine + lax.ppermute(other, C, swap)
    chips = lax.axis_size(CHIPS)
    shape = half.shape
    blocks = half.reshape(chips, -1, 128)
    tiles = lax.all_to_all(blocks, CHIPS, 0, 0, tiled=True)
    own = (jnp.sum(tiles, axis=0) * scaling).astype(BF16)
    own = lax.all_to_all(
        jnp.broadcast_to(own[None], (chips, *own.shape)), CHIPS, 0, 0, tiled=True
    )
    own = own.reshape(shape)
    return own, lax.ppermute(own, C, swap)


def slots_kernel(at, owners, now, prev, *refs):
    outs = refs[:16]
    cells, slot, seen, in_sem, out_sem = refs[16:]
    z, x = at[0], at[1]
    old = now.shape[0]
    first = (z * RING + x) * old
    loads = [
        pltpu.make_async_copy(src, cells.at[a], in_sem.at[a]) for a, src in enumerate((now, prev))
    ]
    for load in loads:
        load.start()
    for d in range(RING * RING):
        seen[d] = 0
        slot[d] = 0
        slot[RING * RING + d] = 0

    def place(i, carry):
        owner = owners[first + i]
        rank = jnp.minimum(seen[owner], 1)
        slot[rank * RING * RING + owner] = i
        seen[owner] = seen[owner] + 1
        return carry

    lax.fori_loop(0, old, place, 0)
    for load in loads:
        load.wait()
    stores = []
    for rank in range(2):
        for kx in range(RING):
            for kz in range(RING):
                d = ((z + kz) & 3) * RING + ((x + kx) & 3)
                i = slot[rank * RING * RING + d]
                n = len(stores)
                stores.append(
                    pltpu.make_async_copy(
                        cells.at[0, i], outs[rank * 8 + kx].at[kz], out_sem.at[n]
                    )
                )
                stores.append(
                    pltpu.make_async_copy(
                        cells.at[1, i], outs[rank * 8 + RING + kz].at[kx], out_sem.at[n + 1]
                    )
                )
    run_copies(stores)


def slots_for_owners(at, owners, now, prev):
    old, rows, nodes = now.shape
    piece = (RING, rows, nodes)
    size = RING * rows * nodes * 2
    return pl.pallas_call(
        slots_kernel,
        out_shape=[sized(piece)] * 16,
        in_specs=[SMEM, SMEM, ANY, ANY],
        out_specs=[ANY] * 16,
        scratch_shapes=[
            pltpu.VMEM((2, old, rows, nodes), BF16),
            pltpu.SMEM((2 * RING * RING,), jnp.int32),
            pltpu.SMEM((RING * RING,), jnp.int32),
            pltpu.SemaphoreType.DMA((2,)),
            pltpu.SemaphoreType.DMA((64,)),
        ],
        cost_estimate=moved(8 * size, 16 * size),
        name="slots_for_owners",
    )(at, owners, now, prev)


def turn_kernel(*refs):
    ins, outs, (buf, in_sem, out_sem) = refs[:4], refs[4:8], refs[8:]
    run_copies(
        [pltpu.make_async_copy(src, buf.at[n], in_sem.at[n]) for n, src in enumerate(ins)]
    )
    run_copies(
        [pltpu.make_async_copy(buf.at[:, n], dst, out_sem.at[n]) for n, dst in enumerate(outs)]
    )


def turned(pieces):
    shape = pieces[0].shape
    size = 4 * math.prod(shape) * 2
    return pl.pallas_call(
        turn_kernel,
        out_shape=[sized(shape)] * RING,
        in_specs=[ANY] * RING,
        out_specs=[ANY] * RING,
        scratch_shapes=[
            pltpu.VMEM((RING, *shape), BF16),
            pltpu.SemaphoreType.DMA((RING,)),
            pltpu.SemaphoreType.DMA((RING,)),
        ],
        cost_estimate=moved(size, size),
        name="turned",
    )(*pieces)


def route_kernel(at, *refs):
    now, prev, outs = refs[:4], refs[4:8], refs[8:16]
    buf, in_sem, out_sem = refs[16:]
    z, x, y, c = at[0], at[1], at[2], at[3]
    run_copies(
        [
            pltpu.make_async_copy(src, buf.at[a, n], in_sem.at[a, n])
            for a, group in enumerate((now, prev))
            for n, src in enumerate(group)
        ]
    )
    stores = []
    for n, (q, l) in enumerate(OFFSETS):
        kz = (z - y - q) & 3
        for e in range(2):
            kx = (x - ((c + l) & 1) * 2 - e) & 3
            stores.append(
                pltpu.make_async_copy(buf.at[0, kz, kx], outs[n].at[0, e], out_sem.at[n, 0, e])
            )
            stores.append(
                pltpu.make_async_copy(buf.at[1, kx, kz], outs[n].at[1, e], out_sem.at[n, 1, e])
            )
    run_copies(stores)


def routed(at, now, prev):
    _, rows, nodes = now[0].shape
    size = 32 * rows * nodes * 2
    return pl.pallas_call(
        route_kernel,
        out_shape=[sized((2, 2, rows, nodes))] * 8,
        in_specs=[SMEM] + [ANY] * 8,
        out_specs=[ANY] * 8,
        scratch_shapes=[
            pltpu.VMEM((2, RING, RING, rows, nodes), BF16),
            pltpu.SemaphoreType.DMA((2, RING)),
            pltpu.SemaphoreType.DMA((8, 2, 2)),
        ],
        cost_estimate=moved(size, size),
        name="routed",
    )(at, *now, *prev)


def predict_kernel(rank, old, at, owners, octants, *refs):
    pieces, mine, other, interp = refs[:8], refs[8], refs[9], refs[10]
    predicted = refs[11 + rank]
    parents, matrices, mix, out, in_sem, mat_sem, mix_sem, out_sem = refs[12 + rank :]
    z, x, y, c = at[0], at[1], at[2], at[3]
    rows = pieces[0].shape[2]
    blocks, half, _ = mine.shape
    owner = z * RING + x
    copies, filled = [], []
    for e in range(2):
        first = (RING * y + 2 * c + e) * old

        def look(i, carry, first=first):
            count, cell = carry
            match = owners[first + i] == owner
            cell = jnp.where(match & (count == rank), i, cell)
            return count + match.astype(jnp.int32), cell

        count, cell = lax.fori_loop(0, old, look, (jnp.int32(0), jnp.int32(0)))
        filled.append(count > rank)
        for j in range(2):
            o = octants[(first + cell) * 2 + j]
            copies.append(
                pltpu.make_async_copy(interp.at[o], matrices.at[e, j], mat_sem.at[e, j])
            )
    for n, (q, l) in enumerate(OFFSETS):
        b = ((y - q) & 3) * CORES + ((c - l) & 1)
        to = pl.ds(pl.multiple_of(b * rows, rows), rows)
        copies.append(pltpu.make_async_copy(pieces[n], parents.at[:, :, to], in_sem.at[n]))
    for n, (side, src) in enumerate(((c, mine), (1 - c, other))):
        u = pl.ds(pl.multiple_of(side * half, half), half)
        for t in range(blocks):
            copies.append(
                pltpu.make_async_copy(
                    src.at[t], mix.at[u, pl.ds(t * 128, 128)], mix_sem.at[n, t]
                )
            )
    run_copies(copies)
    stores = []
    for e in range(2):

        @pl.when(filled[e])
        def _(e=e):
            mixed = jnp.dot(mix[...], parents[0, e], preferred_element_type=F32)
            value = (parents[1, e].astype(F32) + mixed).astype(BF16)
            for j in range(2):
                out[e, j] = lax.dot_general(
                    value, matrices[e, j], (((1,), (1,)), ((), ())), preferred_element_type=F32
                ).astype(BF16)

        @pl.when(jnp.logical_not(filled[e]))
        def _(e=e):
            out[e] = jnp.zeros(out.shape[1:], BF16)

        stores.append(
            pltpu.make_async_copy(
                out.at[e], predicted.at[pl.ds(e * 4 + rank * 2, 2)], out_sem.at[e]
            )
        )
        stores[-1].start()
    for store in stores:
        store.wait()


def predict(rank, old, at, owners, octants, pieces, mine, other, interp, earlier=None):
    _, _, rows, nodes = pieces[0].shape
    states = rows * RING * CORES
    operands = [at, owners, octants, *pieces, mine, other, interp]
    if earlier is not None:
        operands.append(earlier)
    return pl.pallas_call(
        functools.partial(predict_kernel, rank, old),
        out_shape=sized((8, states, nodes)),
        in_specs=[SMEM] * 3 + [ANY] * (len(operands) - 3),
        out_specs=ANY,
        scratch_shapes=[
            pltpu.VMEM((2, 2, states, nodes), BF16),
            pltpu.VMEM((2, 2, nodes, nodes), BF16),
            pltpu.VMEM((states, states), BF16),
            pltpu.VMEM((2, 2, states, nodes), BF16),
            pltpu.SemaphoreType.DMA((8,)),
            pltpu.SemaphoreType.DMA((2, 2)),
            pltpu.SemaphoreType.DMA((2, states // 128)),
            pltpu.SemaphoreType.DMA((2,)),
        ],
        input_output_aliases={} if earlier is None else {len(operands) - 1: 0},
        cost_estimate=moved(5 << 20, 2 << 20, 12 * states * nodes * nodes),
        name=f"predict_{rank}",
    )(*operands)


def per_device(orbitals_now, orbitals_prev, interp, owner_map, child_oct):
    old, rows, nodes = orbitals_now.shape
    states = rows * lax.axis_size(BAND)
    at = jnp.stack([lax.axis_index(a) for a in DOM_BAND]).astype(jnp.int32)
    octants = child_oct.reshape(-1)
    scaling = 1.0 / math.sqrt(2.0 * states * owner_map.shape[0] * nodes)

    sent = cells_for_band(at, orbitals_now, orbitals_prev)
    cells = over_band([sent[0], *sent])[1:]

    slots = slots_for_owners(at, owner_map, orbitals_now, orbitals_prev)
    ranks = []
    for rank in range(2):
        now_x = slots[rank * 8 : rank * 8 + 4]
        prev_z = slots[rank * 8 + 4 : rank * 8 + 8]
        now = round_ring(turned(round_ring(now_x, X)), Z)
        prev = round_ring(turned(round_ring(prev_z, Z)), X)
        ranks.append(over_band(routed(at, now, prev)))

    mine, other = product_of_cells(at, octants, orbitals_now, orbitals_prev, cells, interp)
    mine, other = summed_over_all(mine, other, scaling)

    out = predict(0, old, at, owner_map, octants, ranks[0], mine, other, interp)
    return predict(1, old, at, owner_map, octants, ranks[1], mine, other, interp, out)


def solution(mesh):
    split = Mesh(mesh.devices.reshape(4, 4, 4, 2), DOM_BAND)
    placed = (P(DOM, BAND, None), P(DOM, BAND, None), P(), P(), P())
    return jax.shard_map(
        per_device, mesh=split, in_specs=placed, out_specs=P(DOM_BAND, None, None), check_vma=False
    )
```

```python
import functools
import math

import jax
import jax.numpy as jnp
from jax import lax
from jax.experimental import pallas as pl
from jax.experimental.pallas import tpu as pltpu
from jax.sharding import Mesh
from jax.sharding import PartitionSpec as P


Z, X, Y, C = "dom_0", "dom_1", "band_0", "band_1"
DOM = (Z, X)
BAND = (Y, C)
DOM_BAND = (Z, X, Y, C)
CHIPS = (Z, X, Y)

BF16 = jnp.bfloat16
F32 = jnp.float32
RING = 4
CORES = 2
OFFSETS = tuple((q, l) for q in range(RING) for l in range(CORES))


SMEM = pl.BlockSpec(memory_space=pltpu.SMEM)
ANY = pl.BlockSpec(memory_space=pl.ANY)


def band_pairs(q, l):
    return [
        (y * CORES + c, ((y + q) % RING) * CORES + (c + l) % CORES)
        for y in range(RING)
        for c in range(CORES)
    ]


def over_band(pieces):
    return [
        lax.ppermute(piece, BAND, band_pairs(q, l)) for (q, l), piece in zip(OFFSETS[1:], pieces)
    ]


def run_copies(copies):
    for copy in copies:
        copy.start()
    for copy in copies:
        copy.wait()


def sized(shape, dtype=BF16):
    return jax.ShapeDtypeStruct(shape, dtype)


def moved(read, written, flops=0):
    return pl.CostEstimate(flops=flops, bytes_accessed=read + written, transcendentals=0)


def cells_kernel(at, now, prev, *refs):
    outs, (buf, in_sem, out_sem) = refs[:7], refs[7:]
    y, c = at[2], at[3]
    loads, stores = [], []
    for n, (q, l) in enumerate(OFFSETS[1:]):
        first = (((y + q) & 3) * CORES + ((c + l) & 1)) * 2
        loads.append(
            [
                pltpu.make_async_copy(src.at[pl.ds(first, 2)], buf.at[n, a], in_sem.at[n, a])
                for a, src in enumerate((now, prev))
            ]
        )
        stores.append(pltpu.make_async_copy(buf.at[n], outs[n], out_sem.at[n]))
    for pair in loads:
        for copy in pair:
            copy.start()
    for pair, store in zip(loads, stores):
        for copy in pair:
            copy.wait()
        store.start()
    for store in stores:
        store.wait()


def cells_for_band(at, now, prev):
    _, rows, nodes = now.shape
    piece = (2, 2, rows, nodes)
    size = 4 * rows * nodes * 2
    return pl.pallas_call(
        cells_kernel,
        out_shape=[sized(piece)] * 7,
        in_specs=[SMEM, ANY, ANY],
        out_specs=[ANY] * 7,
        scratch_shapes=[
            pltpu.VMEM((7, *piece), BF16),
            pltpu.SemaphoreType.DMA((7, 2)),
            pltpu.SemaphoreType.DMA((7,)),
        ],
        cost_estimate=moved(7 * size, 7 * size),
        name="cells_for_band",
    )(at, now, prev)


def product_kernel(at, octants, now, prev, *refs):
    pieces, interp, mine, other = refs[:7], refs[7], refs[8], refs[9]
    parents, matrices, kids, out, in_sem, mat_sem, out_sem = refs[10:]
    z, x, y, c = at[0], at[1], at[2], at[3]
    rows = now.shape[1]
    nodes = now.shape[2]
    states = parents.shape[2]
    half = states // 2
    first = (y * CORES + c) * 2
    cell0 = (z * RING + x) * now.shape[0] + first
    copies = []
    for e in range(2):
        for j in range(2):
            o = octants[(cell0 + e) * 2 + j]
            copies.append(
                pltpu.make_async_copy(interp.at[o], matrices.at[e, j], mat_sem.at[e, j])
            )
    own = pl.ds(pl.multiple_of((y * CORES + c) * rows, rows), rows)
    for a, src in enumerate((now, prev)):
        copies.append(
            pltpu.make_async_copy(
                src.at[pl.ds(first, 2)], parents.at[a, :, own], in_sem.at[7 + a]
            )
        )
    for n, (q, l) in enumerate(OFFSETS[1:]):
        b = ((y - q) & 3) * CORES + ((c - l) & 1)
        to = pl.ds(pl.multiple_of(b * rows, rows), rows)
        copies.append(
            pltpu.make_async_copy(pieces[n], parents.at[:, :, to], in_sem.at[n])
        )
    run_copies(copies)
    for a in range(2):
        for e in range(2):
            for j in range(2):
                kids[a, :, pl.ds((e * 2 + j) * nodes, nodes)] = lax.dot_general(
                    parents[a, e],
                    matrices[e, j],
                    (((1,), (1,)), ((), ())),
                    preferred_element_type=F32,
                ).astype(BF16)
    stores = []
    for n, (side, dst) in enumerate(((c, mine), (1 - c, other))):
        u = pl.ds(pl.multiple_of(side * half, half), half)
        part = lax.dot_general(
            kids[1, u, :], kids[0], (((1,), (1,)), ((), ())), preferred_element_type=F32
        )
        for t in range(states // 128):
            out[n, t] = part[:, t * 128 : (t + 1) * 128]
        stores.append(pltpu.make_async_copy(out.at[n], dst, out_sem.at[n]))
        stores[-1].start()
    for store in stores:
        store.wait()


def product_of_cells(at, octants, now, prev, pieces, interp):
    _, rows, nodes = now.shape
    states = rows * RING * CORES
    lanes = (states // 128, states // 2, 128)
    return pl.pallas_call(
        product_kernel,
        out_shape=[sized(lanes, F32)] * 2,
        in_specs=[SMEM, SMEM] + [ANY] * 10,
        out_specs=[ANY] * 2,
        scratch_shapes=[
            pltpu.VMEM((2, 2, states, nodes), BF16),
            pltpu.VMEM((2, 2, nodes, nodes), BF16),
            pltpu.VMEM((2, states, 4 * nodes), BF16),
            pltpu.VMEM((2, *lanes), F32),
            pltpu.SemaphoreType.DMA((9,)),
            pltpu.SemaphoreType.DMA((2, 2)),
            pltpu.SemaphoreType.DMA((2,)),
        ],
        cost_estimate=moved(4 << 20, 1 << 20, 24 * states * nodes * nodes),
        name="product_of_cells",
    )(at, octants, now, prev, *pieces, interp)


def summed_over_all(mine, other, scaling):
    swap = [(0, 1), (1, 0)]
    half = mine + lax.ppermute(other, C, swap)
    chips = lax.axis_size(CHIPS)
    shape = half.shape
    blocks = half.reshape(chips, -1, 128)
    tiles = lax.all_to_all(blocks, CHIPS, 0, 0, tiled=True)
    own = (jnp.sum(tiles, axis=0) * scaling).astype(BF16)
    own = jnp.broadcast_to(own[None], (chips, *own.shape))
    own = lax.all_to_all(own, CHIPS, 0, 0, tiled=True)
    own = own.reshape(shape)
    return own, lax.ppermute(own, C, swap)


def slots_kernel(rank, at, owners, now, prev, out, cells, slot, seen, in_sem, out_sem):
    z, x = at[0], at[1]
    old = now.shape[0]
    first = (z * RING + x) * old
    loads = [
        pltpu.make_async_copy(src, cells.at[a], in_sem.at[a]) for a, src in enumerate((now, prev))
    ]
    for load in loads:
        load.start()
    for d in range(RING * RING):
        seen[d] = 0
        slot[d] = 0

    def place(i, carry):
        owner = owners[first + i]
        slot[owner] = jnp.where(seen[owner] == rank, i, slot[owner])
        seen[owner] = seen[owner] + 1
        return carry

    lax.fori_loop(0, old, place, 0)
    stores = []
    for a in range(2):
        loads[a].wait()
        for d in range(RING * RING):
            stores.append(
                pltpu.make_async_copy(cells.at[a, slot[d]], out.at[d, a], out_sem.at[a, d])
            )
            stores[-1].start()
    for store in stores:
        store.wait()


def slots_for_owners(rank, at, owners, now, prev):
    old, rows, nodes = now.shape
    doms = RING * RING
    size = 2 * old * rows * nodes * 2
    return pl.pallas_call(
        functools.partial(slots_kernel, rank),
        out_shape=sized((doms, 2, rows, nodes)),
        in_specs=[SMEM, SMEM, ANY, ANY],
        out_specs=ANY,
        scratch_shapes=[
            pltpu.VMEM((2, old, rows, nodes), BF16),
            pltpu.SMEM((doms,), jnp.int32),
            pltpu.SMEM((doms,), jnp.int32),
            pltpu.SemaphoreType.DMA((2,)),
            pltpu.SemaphoreType.DMA((2, doms)),
        ],
        cost_estimate=moved(size, size),
    )(at, owners, now, prev)


def route_kernel(at, slots, *refs):
    outs, (buf, in_sem, out_sem) = refs[:7], refs[7:]
    y, c = at[2], at[3]
    loads, stores = [], []
    for n, (q, l) in enumerate(OFFSETS[1:]):
        first = (((y + q) & 3) * CORES + ((c + l) & 1)) * 2
        loads.append(pltpu.make_async_copy(slots.at[pl.ds(first, 2)], buf.at[n], in_sem.at[n]))
        stores.append(pltpu.make_async_copy(buf.at[n], outs[n], out_sem.at[n]))
    for load in loads:
        load.start()
    for load, store in zip(loads, stores):
        load.wait()
        store.start()
    for store in stores:
        store.wait()


def routed(at, slots):
    piece = (2, *slots.shape[1:])
    size = 7 * math.prod(piece) * 2
    return pl.pallas_call(
        route_kernel,
        out_shape=[sized(piece)] * 7,
        in_specs=[SMEM, ANY],
        out_specs=[ANY] * 7,
        scratch_shapes=[
            pltpu.VMEM((7, *piece), BF16),
            pltpu.SemaphoreType.DMA((7,)),
            pltpu.SemaphoreType.DMA((7,)),
        ],
        cost_estimate=moved(size, size),
    )(at, slots)


def predict_kernel(rank, old, at, owners, octants, *refs):
    slots, pieces, mine, other, interp = refs[0], refs[1:8], refs[8], refs[9], refs[10]
    predicted = refs[11 + rank]
    parents, matrices, mix, out, in_sem, mat_sem, mix_sem, out_sem = refs[12 + rank :]
    z, x, y, c = at[0], at[1], at[2], at[3]
    rows = pieces[0].shape[2]
    blocks, half, _ = mine.shape
    owner = z * RING + x
    copies, filled = [], []
    for e in range(2):
        first = (RING * y + 2 * c + e) * old

        def look(i, carry, first=first):
            count, cell = carry
            match = owners[first + i] == owner
            cell = jnp.where(match & (count == rank), i, cell)
            return count + match.astype(jnp.int32), cell

        count, cell = lax.fori_loop(0, old, look, (jnp.int32(0), jnp.int32(0)))
        filled.append(count > rank)
        for j in range(2):
            o = octants[(first + cell) * 2 + j]
            copies.append(
                pltpu.make_async_copy(interp.at[o], matrices.at[e, j], mat_sem.at[e, j])
            )
    for n, (q, l) in enumerate(OFFSETS):
        b = ((y - q) & 3) * CORES + ((c - l) & 1)
        to = pl.ds(pl.multiple_of(b * rows, rows), rows)
        src = pieces[n - 1] if n else slots.at[pl.ds(b * 2, 2)]
        copies.append(pltpu.make_async_copy(src, parents.at[:, :, to], in_sem.at[n]))
    for n, (side, src) in enumerate(((c, mine), (1 - c, other))):
        u = pl.ds(pl.multiple_of(side * half, half), half)
        for t in range(blocks):
            copies.append(
                pltpu.make_async_copy(
                    src.at[t], mix.at[u, pl.ds(t * 128, 128)], mix_sem.at[n, t]
                )
            )
    run_copies(copies)
    stores = []
    for e in range(2):

        @pl.when(filled[e])
        def _(e=e):
            mixed = jnp.dot(mix[...], parents[e, 0], preferred_element_type=F32)
            value = (parents[e, 1].astype(F32) + mixed).astype(BF16)
            for j in range(2):
                out[e, j] = lax.dot_general(
                    value, matrices[e, j], (((1,), (1,)), ((), ())), preferred_element_type=F32
                ).astype(BF16)

        @pl.when(jnp.logical_not(filled[e]))
        def _(e=e):
            out[e] = jnp.zeros(out.shape[1:], BF16)

        stores.append(
            pltpu.make_async_copy(
                out.at[e], predicted.at[pl.ds(e * 4 + rank * 2, 2)], out_sem.at[e]
            )
        )
        stores[-1].start()
    for store in stores:
        store.wait()


def predict(rank, old, at, owners, octants, slots, pieces, mine, other, interp, earlier=None):
    _, _, rows, nodes = pieces[0].shape
    states = rows * RING * CORES
    operands = [at, owners, octants, slots, *pieces, mine, other, interp]
    if earlier is not None:
        operands.append(earlier)
    return pl.pallas_call(
        functools.partial(predict_kernel, rank, old),
        out_shape=sized((8, states, nodes)),
        in_specs=[SMEM] * 3 + [ANY] * (len(operands) - 3),
        out_specs=ANY,
        scratch_shapes=[
            pltpu.VMEM((2, 2, states, nodes), BF16),
            pltpu.VMEM((2, 2, nodes, nodes), BF16),
            pltpu.VMEM((states, states), BF16),
            pltpu.VMEM((2, 2, states, nodes), BF16),
            pltpu.SemaphoreType.DMA((8,)),
            pltpu.SemaphoreType.DMA((2, 2)),
            pltpu.SemaphoreType.DMA((2, states // 128)),
            pltpu.SemaphoreType.DMA((2,)),
        ],
        input_output_aliases={} if earlier is None else {len(operands) - 1: 0},
        cost_estimate=moved(5 << 20, 2 << 20, 12 * states * nodes * nodes),
    )(*operands)


def refined(orbitals_now, orbitals_prev, interp, owner_map, child_oct):
    old, rows, nodes = orbitals_now.shape
    states = rows * lax.axis_size(BAND)
    at = jnp.stack([lax.axis_index(a) for a in DOM_BAND]).astype(jnp.int32)
    octants = child_oct.reshape(-1)
    scaling = 1.0 / math.sqrt(2.0 * states * owner_map.shape[0] * nodes)

    slots, pieces = [], []
    for rank in range(2):
        slots.append(slots_for_owners(rank, at, owner_map, orbitals_now, orbitals_prev))
        slots[rank] = lax.all_to_all(slots[rank], DOM, 0, 0, tiled=True)
        pieces.append(routed(at, slots[rank]))
        pieces[rank] = over_band(pieces[rank])

    cells = cells_for_band(at, orbitals_now, orbitals_prev)
    cells = over_band(cells)
    mine, other = product_of_cells(at, octants, orbitals_now, orbitals_prev, cells, interp)
    mine, other = summed_over_all(mine, other, scaling)

    out = predict(0, old, at, owner_map, octants, slots[0], pieces[0], mine, other, interp)
    return predict(1, old, at, owner_map, octants, slots[1], pieces[1], mine, other, interp, out)


def solution(mesh):
    split = Mesh(mesh.devices.reshape(4, 4, 4, 2), DOM_BAND)
    placed = (P(DOM, BAND, None), P(DOM, BAND, None), P(), P(), P())
    return jax.shard_map(
        refined, mesh=split, in_specs=placed, out_specs=P(DOM_BAND, None, None), check_vma=False
    )
```

```python
import functools
import math

import jax
import jax.numpy as jnp
from jax import lax
from jax.experimental import pallas as pl
from jax.experimental.pallas import tpu as pltpu
from jax.sharding import Mesh
from jax.sharding import PartitionSpec as P


Z, X, Y, C = "dom_0", "dom_1", "band_0", "band_1"
DOM = (Z, X)
BAND = (Y, C)
DOM_BAND = (Z, X, Y, C)
CHIPS = (Z, X, Y)

BF16 = jnp.bfloat16
F32 = jnp.float32
RING = 4
CORES = 2
OFFSETS = tuple((q, l) for q in range(RING) for l in range(CORES))


WHOLE_VMEM = pltpu.CompilerParams(vmem_limit_bytes=67_043_328)

SMEM = pl.BlockSpec(memory_space=pltpu.SMEM)
HBM = pl.BlockSpec(memory_space=pltpu.HBM)


def band_pairs(q, l):
    return [
        (y * CORES + c, ((y + q) % RING) * CORES + (c + l) % CORES)
        for y in range(RING)
        for c in range(CORES)
    ]


def over_band(pieces):
    return [
        lax.ppermute(piece, BAND, band_pairs(q, l)) for (q, l), piece in zip(OFFSETS[1:], pieces)
    ]


def sized(shape, dtype=BF16):
    return jax.ShapeDtypeStruct(shape, dtype)


def moved(read, written, flops=0):
    return pl.CostEstimate(flops=flops, bytes_accessed=read + written, transcendentals=0)


def cells_kernel(at, now, prev, *refs):
    outs, (buf, in_sem, out_sem) = refs[:7], refs[7:]
    y, c = at[2], at[3]
    loads, stores = [], []
    for n, (q, l) in enumerate(OFFSETS[1:]):
        first = (((y + q) & 3) * CORES + ((c + l) & 1)) * 2
        loads.append(
            [
                pltpu.make_async_copy(src.at[pl.ds(first, 2)], buf.at[n, a], in_sem.at[n, a])
                for a, src in enumerate((now, prev))
            ]
        )
        stores.append(pltpu.make_async_copy(buf.at[n], outs[n], out_sem.at[n]))
    for pair in loads:
        for copy in pair:
            copy.start()
    for pair, store in zip(loads, stores):
        for copy in pair:
            copy.wait()
        store.start()
    for store in stores:
        store.wait()


def cells_for_band(at, now, prev):
    _, rows, nodes = now.shape
    piece = (2, 2, rows, nodes)
    size = 4 * rows * nodes * 2
    return pl.pallas_call(
        cells_kernel,
        out_shape=[sized(piece)] * 7,
        in_specs=[SMEM, HBM, HBM],
        out_specs=[HBM] * 7,
        scratch_shapes=[
            pltpu.VMEM((7, *piece), BF16),
            pltpu.SemaphoreType.DMA((7, 2)),
            pltpu.SemaphoreType.DMA((7,)),
        ],
        compiler_params=WHOLE_VMEM,
        cost_estimate=moved(7 * size, 7 * size),
        name="cells_for_band",
    )(at, now, prev)


def product_kernel(at, octants, now, prev, *refs):
    pieces, interp, mine, other = refs[:7], refs[7], refs[8:12], refs[12]
    parents, matrices, kids, out, in_sem, mat_sem, out_sem = refs[13:]
    z, x, y, c = at[0], at[1], at[2], at[3]
    rows = now.shape[1]
    nodes = now.shape[2]
    states = parents.shape[2]
    half = states // 2
    first = (y * CORES + c) * 2
    cell0 = (z * RING + x) * now.shape[0] + first
    loads = []
    for e in range(2):
        copies = []
        for a, src in enumerate((now, prev)):
            own = pl.ds(pl.multiple_of((y * CORES + c) * rows, rows), rows)
            copies.append(
                pltpu.make_async_copy(
                    src.at[first + e], parents.at[a, e, own], in_sem.at[e, 7 + a]
                )
            )
        for n, (q, l) in enumerate(OFFSETS[1:]):
            b = ((y - q) & 3) * CORES + ((c - l) & 1)
            to = pl.ds(pl.multiple_of(b * rows, rows), rows)
            copies.append(
                pltpu.make_async_copy(
                    pieces[n].at[:, e], parents.at[:, e, to], in_sem.at[e, n]
                )
            )
        for j in range(2):
            o = octants[(cell0 + e) * 2 + j]
            copies.append(
                pltpu.make_async_copy(interp.at[o], matrices.at[e, j], mat_sem.at[e, j])
            )
        for copy in copies:
            copy.start()
        loads.append(copies)
    for e in range(2):
        for copy in loads[e]:
            copy.wait()
        for a in range(2):
            for j in range(2):
                kids[a, :, pl.ds((e * 2 + j) * nodes, nodes)] = lax.dot_general(
                    parents[a, e],
                    matrices[e, j],
                    (((1,), (1,)), ((), ())),
                    preferred_element_type=F32,
                ).astype(BF16)
    stores = []
    for n, side in enumerate((1 - c, c)):
        u = pl.ds(pl.multiple_of(side * half, half), half)
        part = lax.dot_general(
            kids[1, u, :], kids[0], (((1,), (1,)), ((), ())), preferred_element_type=F32
        )
        for t in range(RING):
            out[n, t] = part[:, t * 128 : (t + 1) * 128]
        for k in range(RING):
            dst = mine[k] if n else other.at[k]
            stores.append(pltpu.make_async_copy(out.at[n, (y + k) & 3], dst, out_sem.at[n, k]))
            stores[-1].start()
    for store in stores:
        store.wait()


def product_of_cells(at, octants, now, prev, pieces, interp):
    _, rows, nodes = now.shape
    states = rows * RING * CORES
    block = (states // 2, 128)
    return pl.pallas_call(
        product_kernel,
        out_shape=[sized(block, F32)] * RING + [sized((RING, *block), F32)],
        in_specs=[SMEM, SMEM] + [HBM] * 10,
        out_specs=[HBM] * 5,
        scratch_shapes=[
            pltpu.VMEM((2, 2, states, nodes), BF16),
            pltpu.VMEM((2, 2, nodes, nodes), BF16),
            pltpu.VMEM((2, states, 4 * nodes), BF16),
            pltpu.VMEM((2, RING, *block), F32),
            pltpu.SemaphoreType.DMA((2, 9)),
            pltpu.SemaphoreType.DMA((2, 2)),
            pltpu.SemaphoreType.DMA((2, RING)),
        ],
        compiler_params=WHOLE_VMEM,
        cost_estimate=moved(4 << 20, 1 << 20, 24 * states * nodes * nodes),
        name="product_of_cells",
    )(at, octants, now, prev, *pieces, interp)


def summed_over_all(mine, other, scaling):
    swap = [(0, 1), (1, 0)]
    other = lax.ppermute(other, C, swap)
    blocks = [block + other[k] for k, block in enumerate(mine)]
    blocks[1:] = [
        lax.ppermute(blocks[k], Y, [(i, (i + k) % RING) for i in range(RING)])
        for k in range(1, RING)
    ]
    block = (blocks[0] + blocks[1]) + (blocks[2] + blocks[3])
    doms = lax.axis_size(DOM)
    tiles = lax.all_to_all(block.reshape(doms, -1, 128), DOM, 0, 0, tiled=True)
    own = (jnp.sum(tiles, axis=0) * scaling).astype(BF16)
    own = jnp.broadcast_to(own[None], (doms * RING, *own.shape))
    own = lax.all_to_all(own, CHIPS, 0, 0, tiled=True)
    own = own.reshape(doms, RING, -1, 128)
    return own, lax.ppermute(own, C, swap)


def slots_kernel(rank, at, owners, now, prev, out, cells, slot, seen, in_sem, out_sem):
    z, x = at[0], at[1]
    old = now.shape[0]
    first = (z * RING + x) * old
    loads = [
        pltpu.make_async_copy(src, cells.at[a], in_sem.at[a]) for a, src in enumerate((now, prev))
    ]
    for load in loads:
        load.start()
    for d in range(RING * RING):
        seen[d] = 0
        slot[d] = 0

    def place(i, carry):
        owner = owners[first + i]
        slot[owner] = jnp.where(seen[owner] == rank, i, slot[owner])
        seen[owner] = seen[owner] + 1
        return carry

    lax.fori_loop(0, old, place, 0)
    stores = []
    for a in range(2):
        loads[a].wait()
        for d in range(RING * RING):
            stores.append(
                pltpu.make_async_copy(cells.at[a, slot[d]], out.at[d, a], out_sem.at[a, d])
            )
            stores[-1].start()
    for store in stores:
        store.wait()


def slots_for_owners(rank, at, owners, now, prev):
    old, rows, nodes = now.shape
    doms = RING * RING
    size = 2 * old * rows * nodes * 2
    return pl.pallas_call(
        functools.partial(slots_kernel, rank),
        out_shape=sized((doms, 2, rows, nodes)),
        in_specs=[SMEM, SMEM, HBM, HBM],
        out_specs=HBM,
        scratch_shapes=[
            pltpu.VMEM((2, old, rows, nodes), BF16),
            pltpu.SMEM((doms,), jnp.int32),
            pltpu.SMEM((doms,), jnp.int32),
            pltpu.SemaphoreType.DMA((2,)),
            pltpu.SemaphoreType.DMA((2, doms)),
        ],
        compiler_params=WHOLE_VMEM,
        cost_estimate=moved(size, size),
    )(at, owners, now, prev)


def route_kernel(at, slots, *refs):
    outs, (buf, in_sem, out_sem) = refs[:7], refs[7:]
    y, c = at[2], at[3]
    loads, stores = [], []
    for n, (q, l) in enumerate(OFFSETS[1:]):
        first = (((y + q) & 3) * CORES + ((c + l) & 1)) * 2
        loads.append(pltpu.make_async_copy(slots.at[pl.ds(first, 2)], buf.at[n], in_sem.at[n]))
        stores.append(pltpu.make_async_copy(buf.at[n], outs[n], out_sem.at[n]))
    for load in loads:
        load.start()
    for load, store in zip(loads, stores):
        load.wait()
        store.start()
    for store in stores:
        store.wait()


def routed(at, slots):
    piece = (2, *slots.shape[1:])
    size = 7 * math.prod(piece) * 2
    return pl.pallas_call(
        route_kernel,
        out_shape=[sized(piece)] * 7,
        in_specs=[SMEM, HBM],
        out_specs=[HBM] * 7,
        scratch_shapes=[
            pltpu.VMEM((7, *piece), BF16),
            pltpu.SemaphoreType.DMA((7,)),
            pltpu.SemaphoreType.DMA((7,)),
        ],
        compiler_params=WHOLE_VMEM,
        cost_estimate=moved(size, size),
    )(at, slots)


def predict_kernel(old, at, owners, octants, *refs):
    slots, mine, other, interp, predicted = (refs[0], refs[8]), *refs[16:20]
    pieces = (refs[1:8], refs[9:16])
    parents, matrices, mix, out, in_sem, mat_sem, mix_sem, out_sem = refs[20:]
    z, x, y, c = at[0], at[1], at[2], at[3]
    rows = slots[0].shape[2]
    states = parents.shape[2]
    blocks = mine.shape[0]
    owner = z * RING + x
    mixing = []
    for n, (side, src) in enumerate(((c, mine), (1 - c, other))):
        u = pl.ds(side * blocks, blocks)
        for t in range(RING):
            mixing.append(
                pltpu.make_async_copy(
                    src.at[:, t], mix.at[u, :, pl.ds(t * 128, 128)], mix_sem.at[n, t]
                )
            )
    for copy in mixing:
        copy.start()
    loads, filled = [], []
    for k in range(4):
        rank, e = k // 2, k % 2
        first = (RING * y + 2 * c + e) * old

        def look(i, carry, first=first, rank=rank):
            count, cell = carry
            match = owners[first + i] == owner
            cell = jnp.where(match & (count == rank), i, cell)
            return count + match.astype(jnp.int32), cell

        count, cell = lax.fori_loop(0, old, look, (jnp.int32(0), jnp.int32(0)))
        filled.append(count > rank)
        copies = []
        for n, (q, l) in enumerate(OFFSETS):
            b = ((y - q) & 3) * CORES + ((c - l) & 1)
            to = pl.ds(pl.multiple_of(b * rows, rows), rows)
            src = pieces[rank][n - 1].at[e] if n else slots[rank].at[b * 2 + e]
            copies.append(pltpu.make_async_copy(src, parents.at[k, :, to], in_sem.at[k, n]))
        for j in range(2):
            o = octants[(first + cell) * 2 + j]
            copies.append(
                pltpu.make_async_copy(interp.at[o], matrices.at[k, j], mat_sem.at[k, j])
            )
        for copy in copies:
            copy.start()
        loads.append(copies)
    for copy in mixing:
        copy.wait()
    stores = []
    for k in range(4):
        rank, e = k // 2, k % 2
        for copy in loads[k]:
            copy.wait()

        @pl.when(filled[k])
        def _(k=k):
            mixed = jnp.dot(
                mix[...].reshape(states, states), parents[k, 0], preferred_element_type=F32
            )
            value = (parents[k, 1].astype(F32) + mixed).astype(BF16)
            for j in range(2):
                out[k, j] = lax.dot_general(
                    value, matrices[k, j], (((1,), (1,)), ((), ())), preferred_element_type=F32
                ).astype(BF16)

        @pl.when(jnp.logical_not(filled[k]))
        def _(k=k):
            out[k] = jnp.zeros(out.shape[1:], BF16)

        stores.append(
            pltpu.make_async_copy(
                out.at[k], predicted.at[pl.ds(e * 4 + rank * 2, 2)], out_sem.at[k]
            )
        )
        stores[-1].start()
    for store in stores:
        store.wait()


def predict(old, at, owners, octants, slots, pieces, mine, other, interp):
    _, _, rows, nodes = slots[0].shape
    states = rows * RING * CORES
    return pl.pallas_call(
        functools.partial(predict_kernel, old),
        out_shape=sized((8, states, nodes)),
        in_specs=[SMEM] * 3 + [HBM] * 19,
        out_specs=HBM,
        scratch_shapes=[
            pltpu.VMEM((4, 2, states, nodes), BF16),
            pltpu.VMEM((4, 2, nodes, nodes), BF16),
            pltpu.VMEM((states // 16, 16, states), BF16),
            pltpu.VMEM((4, 2, states, nodes), BF16),
            pltpu.SemaphoreType.DMA((4, 8)),
            pltpu.SemaphoreType.DMA((4, 2)),
            pltpu.SemaphoreType.DMA((2, RING)),
            pltpu.SemaphoreType.DMA((4,)),
        ],
        compiler_params=WHOLE_VMEM,
        cost_estimate=moved(9 << 20, 4 << 20, 24 * states * nodes * nodes),
        name="predict",
    )(at, owners, octants, slots[0], *pieces[0], slots[1], *pieces[1], mine, other, interp)


def refined(orbitals_now, orbitals_prev, interp, owner_map, child_oct):
    old, rows, nodes = orbitals_now.shape
    states = rows * lax.axis_size(BAND)
    at = jnp.stack([lax.axis_index(a) for a in DOM_BAND]).astype(jnp.int32)
    octants = child_oct.reshape(-1)
    scaling = 1.0 / math.sqrt(2.0 * states * owner_map.shape[0] * nodes)

    slots, pieces = [], []
    for rank in range(2):
        slots.append(slots_for_owners(rank, at, owner_map, orbitals_now, orbitals_prev))
        slots[rank] = lax.all_to_all(slots[rank], DOM, 0, 0, tiled=True)
        pieces.append(routed(at, slots[rank]))
        pieces[rank] = over_band(pieces[rank])

    cells = cells_for_band(at, orbitals_now, orbitals_prev)
    cells = over_band(cells)
    *mine, other = product_of_cells(at, octants, orbitals_now, orbitals_prev, cells, interp)
    mine, other = summed_over_all(mine, other, scaling)

    return predict(old, at, owner_map, octants, slots, pieces, mine, other, interp)


def solution(mesh):
    split = Mesh(mesh.devices.reshape(4, 4, 4, 2), DOM_BAND)
    placed = (P(DOM, BAND, None), P(DOM, BAND, None), P(), P(), P())
    return jax.shard_map(
        refined, mesh=split, in_specs=placed, out_specs=P(DOM_BAND, None, None), check_vma=False
    )
```

```python
import functools
import math

import jax
import jax.numpy as jnp
from jax import lax
from jax.experimental import pallas as pl
from jax.experimental.pallas import tpu as pltpu
from jax.sharding import Mesh
from jax.sharding import PartitionSpec as P


Z, X, Y, C = "dom_0", "dom_1", "band_0", "band_1"
DOM = (Z, X)
BAND = (Y, C)
DOM_BAND = (Z, X, Y, C)
CHIPS = (Z, X, Y)

BF16 = jnp.bfloat16
F32 = jnp.float32
RING = 4
CORES = 2
UNIT = 16
OFFSETS = ((0, 0), (1, 0), (3, 0), (2, 0), (1, 1), (3, 1), (2, 1), (0, 1))


WHOLE_VMEM = pltpu.CompilerParams(vmem_limit_bytes=67_043_328)

SMEM = pl.BlockSpec(memory_space=pltpu.SMEM)
HBM = pl.BlockSpec(memory_space=pltpu.HBM)


def band_pairs(q, l):
    return [
        (y * CORES + c, ((y + q) % RING) * CORES + (c + l) % CORES)
        for y in range(RING)
        for c in range(CORES)
    ]


def over_band(pieces):
    return [
        lax.ppermute(piece, BAND, band_pairs(q, l)) for (q, l), piece in zip(OFFSETS[1:], pieces)
    ]


def sized(shape, dtype=BF16):
    return jax.ShapeDtypeStruct(shape, dtype)


def moved(read, written, flops=0):
    return pl.CostEstimate(flops=flops, bytes_accessed=read + written, transcendentals=0)


def cells_kernel(at, now, prev, *refs):
    outs, (buf, in_sem, out_sem) = refs[:7], refs[7:]
    y, c = at[2], at[3]
    loads, stores = [], []
    for n, (q, l) in enumerate(OFFSETS[1:]):
        first = (((y + q) & 3) * CORES + ((c + l) & 1)) * 2
        loads.append(
            [
                pltpu.make_async_copy(src.at[pl.ds(first, 2)], buf.at[n, a], in_sem.at[n, a])
                for a, src in enumerate((now, prev))
            ]
        )
        stores.append(pltpu.make_async_copy(buf.at[n], outs[n], out_sem.at[n]))
    for pair in loads:
        for copy in pair:
            copy.start()
    for pair, store in zip(loads, stores):
        for copy in pair:
            copy.wait()
        store.start()
    for store in stores:
        store.wait()


def cells_for_band(at, now, prev):
    _, rows, nodes = now.shape
    piece = (2, 2, rows, nodes)
    size = 4 * rows * nodes * 2
    return pl.pallas_call(
        cells_kernel,
        out_shape=[sized(piece)] * 7,
        in_specs=[SMEM, HBM, HBM],
        out_specs=[HBM] * 7,
        scratch_shapes=[
            pltpu.VMEM((7, *piece), BF16),
            pltpu.SemaphoreType.DMA((7, 2)),
            pltpu.SemaphoreType.DMA((7,)),
        ],
        compiler_params=WHOLE_VMEM,
        cost_estimate=moved(7 * size, 7 * size),
        name="cells_for_band",
    )(at, now, prev)


def product_kernel(at, octants, now, prev, *refs):
    pieces, interp, mine, other = refs[:7], refs[7], refs[8], refs[9]
    parents, matrices, kids, out, in_sem, mat_sem, out_sem = refs[10:]
    z, x, y, c = at[0], at[1], at[2], at[3]
    rows = now.shape[1]
    nodes = now.shape[2]
    states = parents.shape[2]
    half = states // 2
    first = (y * CORES + c) * 2
    cell0 = (z * RING + x) * now.shape[0] + first
    loads = []
    for e in range(2):
        copies = []
        for a, src in enumerate((now, prev)):
            own = pl.ds(pl.multiple_of((y * CORES + c) * rows, rows), rows)
            copies.append(
                pltpu.make_async_copy(
                    src.at[first + e], parents.at[a, e, own], in_sem.at[e, 7 + a]
                )
            )
        for n, (q, l) in enumerate(OFFSETS[1:]):
            b = ((y - q) & 3) * CORES + ((c - l) & 1)
            to = pl.ds(pl.multiple_of(b * rows, rows), rows)
            copies.append(
                pltpu.make_async_copy(
                    pieces[n].at[:, e], parents.at[:, e, to], in_sem.at[e, n]
                )
            )
        for j in range(2):
            o = octants[(cell0 + e) * 2 + j]
            copies.append(
                pltpu.make_async_copy(interp.at[o], matrices.at[e, j], mat_sem.at[e, j])
            )
        for copy in copies:
            copy.start()
        loads.append(copies)
    for e in range(2):
        for copy in loads[e]:
            copy.wait()
        for a in range(2):
            for j in range(2):
                kids[a, :, pl.ds((e * 2 + j) * nodes, nodes)] = lax.dot_general(
                    parents[a, e],
                    matrices[e, j],
                    (((1,), (1,)), ((), ())),
                    preferred_element_type=F32,
                ).astype(BF16)
    stores = []
    for n, side in enumerate((1 - c, c)):
        u = pl.ds(pl.multiple_of(side * half, half), half)
        part = lax.dot_general(
            kids[1, u, :], kids[0], (((1,), (1,)), ((), ())), preferred_element_type=F32
        )
        for t in range(states // 128):
            out[n, t] = part[:, t * 128 : (t + 1) * 128]
        stores.append(pltpu.make_async_copy(out.at[n], mine if n else other, out_sem.at[n]))
        stores[-1].start()
    for store in stores:
        store.wait()


def product_of_cells(at, octants, now, prev, pieces, interp):
    _, rows, nodes = now.shape
    states = rows * RING * CORES
    lanes = (states // 128, states // 2, 128)
    return pl.pallas_call(
        product_kernel,
        out_shape=[sized(lanes, F32)] * 2,
        in_specs=[SMEM, SMEM] + [HBM] * 10,
        out_specs=[HBM] * 2,
        scratch_shapes=[
            pltpu.VMEM((2, 2, states, nodes), BF16),
            pltpu.VMEM((2, 2, nodes, nodes), BF16),
            pltpu.VMEM((2, states, 4 * nodes), BF16),
            pltpu.VMEM((2, *lanes), F32),
            pltpu.SemaphoreType.DMA((2, 9)),
            pltpu.SemaphoreType.DMA((2, 2)),
            pltpu.SemaphoreType.DMA((2,)),
        ],
        compiler_params=WHOLE_VMEM,
        cost_estimate=moved(4 << 20, 1 << 20, 24 * states * nodes * nodes),
        name="product_of_cells",
    )(at, octants, now, prev, *pieces, interp)


def summed_over_all(mine, other, scaling):
    swap = [(0, 1), (1, 0)]
    half = mine + lax.ppermute(other, C, swap)
    chips = lax.axis_size(CHIPS)
    tiles = lax.all_to_all(half.reshape(chips, -1, 128), CHIPS, 0, 0, tiled=True)
    own = (jnp.sum(tiles, axis=0) * scaling).astype(BF16)
    own = jnp.stack([own, lax.ppermute(own, C, swap)])
    own = jnp.broadcast_to(own[None], (chips // RING, *own.shape))
    own = lax.all_to_all(own, DOM, 0, 0, tiled=True)
    own = own.reshape(RING, RING, *own.shape[1:])
    return [own] + [
        lax.ppermute(own, Y, [(i, (i + k) % RING) for i in range(RING)])
        for k in range(1, RING)
    ]


def slots_kernel(parts, owners, octants, now, prev, out, cells, slot, seen, in_sem, out_sem):
    z, x = lax.axis_index(Z), lax.axis_index(X)
    old = now.shape[0]
    doms = RING * RING
    first = (z * RING + x) * old
    loads = [
        pltpu.make_async_copy(src, cells.at[a], in_sem.at[a]) for a, src in enumerate((now, prev))
    ]
    for load in loads:
        load.start()
    for d in range(doms):
        seen[d] = 0
        for rank in range(2):
            slot[rank * doms + d] = 0

    def place(i, carry):
        owner = owners[first + i]
        rank = jnp.minimum(seen[owner], 1)
        slot[rank * doms + owner] = i
        seen[owner] = rank + 1
        return carry

    lax.fori_loop(0, old, place, 0)
    stores = []
    for a in range(2):
        loads[a].wait()
        at_unit = 0
        for n, (rank, begin, units) in enumerate(parts):
            for d in range(doms):
                stores.append(
                    pltpu.make_async_copy(
                        cells.at[a, slot[rank * doms + d], pl.ds(begin, units)],
                        out.at[d, pl.ds(at_unit, units), a],
                        out_sem.at[n, a, d],
                    )
                )
                stores[-1].start()
            at_unit += units
    for store in stores:
        store.wait()


def slots_for_owners(parts, owners, octants, now, prev):
    old, units, _, nodes = now.shape
    doms = RING * RING
    total = sum(n for _, _, n in parts)
    size = 2 * doms * total * UNIT * nodes * 2
    return pl.pallas_call(
        functools.partial(slots_kernel, parts),
        out_shape=sized((doms, total, 2, UNIT, nodes)),
        in_specs=[SMEM, SMEM, HBM, HBM],
        out_specs=HBM,
        scratch_shapes=[
            pltpu.VMEM((2, old, units, UNIT, nodes), BF16),
            pltpu.SMEM((2 * doms,), jnp.int32),
            pltpu.SMEM((doms,), jnp.int32),
            pltpu.SemaphoreType.DMA((2,)),
            pltpu.SemaphoreType.DMA((len(parts), 2, doms)),
        ],
        compiler_params=WHOLE_VMEM,
        cost_estimate=moved(size, size),
    )(owners, octants, now, prev)


def route_kernel(at, slots, *refs):
    outs, (buf, in_sem, out_sem) = refs[:7], refs[7:]
    y, c = at[2], at[3]
    loads, stores = [], []
    for n, (q, l) in enumerate(OFFSETS[1:]):
        first = (((y + q) & 3) * CORES + ((c + l) & 1)) * 2
        loads.append(pltpu.make_async_copy(slots.at[pl.ds(first, 2)], buf.at[n], in_sem.at[n]))
        stores.append(pltpu.make_async_copy(buf.at[n], outs[n], out_sem.at[n]))
    for load in loads:
        load.start()
    for load, store in zip(loads, stores):
        load.wait()
        store.start()
    for store in stores:
        store.wait()


def routed(at, slots):
    piece = (2, *slots.shape[1:])
    size = 7 * math.prod(piece) * 2
    return pl.pallas_call(
        route_kernel,
        out_shape=[sized(piece)] * 7,
        in_specs=[SMEM, HBM],
        out_specs=[HBM] * 7,
        scratch_shapes=[
            pltpu.VMEM((7, *piece), BF16),
            pltpu.SemaphoreType.DMA((7,)),
            pltpu.SemaphoreType.DMA((7,)),
        ],
        compiler_params=WHOLE_VMEM,
        cost_estimate=moved(size, size),
    )(at, slots)


def predict_kernel(old, at, owners, octants, *refs):
    slots, pieces = (refs[0], refs[8]), (refs[1:8], refs[9:16])
    tiles, interp, predicted = refs[16:20], refs[20], refs[21]
    parents, matrices, planes, mix, out, in_sem, mat_sem, mix_sem, out_sem = refs[22:]
    z, x, y, c = at[0], at[1], at[2], at[3]
    units = parents.shape[1] // (RING * CORES)
    nodes = parents.shape[4]
    states = parents.shape[1] * UNIT
    owner = z * RING + x
    mixing = []
    for n, side in enumerate((c, 1 - c)):
        for k in range(RING):
            to = planes.at[:, side, :, (y - k) & 3]
            mixing.append(pltpu.make_async_copy(tiles[k].at[:, :, n], to, mix_sem.at[n, k]))
    for copy in mixing:
        copy.start()
    loads, filled = [], []
    for k in range(4):
        rank, e = k // 2, k % 2
        first = (RING * y + 2 * c + e) * old

        def look(i, carry, first=first, rank=rank):
            count, cell = carry
            match = owners[first + i] == owner
            cell = jnp.where(match & (count == rank), i, cell)
            return count + match.astype(jnp.int32), cell

        count, cell = lax.fori_loop(0, old, look, (jnp.int32(0), jnp.int32(0)))
        filled.append(count > rank)
        copies = []
        for n, (q, l) in enumerate(OFFSETS):
            b = ((y - q) & 3) * CORES + ((c - l) & 1)
            src = pieces[rank][n - 1].at[e] if n else slots[rank].at[b * 2 + e]
            to = parents.at[k, pl.ds(b * units, units)]
            copies.append(pltpu.make_async_copy(src, to, in_sem.at[k, n]))
        for j in range(2):
            o = octants[(first + cell) * 2 + j]
            copies.append(
                pltpu.make_async_copy(interp.at[o], matrices.at[k, j], mat_sem.at[k, j])
            )
        for copy in copies:
            copy.start()
        loads.append(copies)
    for copy in mixing:
        copy.wait()
    for t in range(RING):
        mix[:, pl.ds(t * 128, 128)] = planes[t].reshape(states, 128)
    stores = []
    for k in range(4):
        rank, e = k // 2, k % 2
        for copy in loads[k]:
            copy.wait()

        @pl.when(filled[k])
        def _(k=k):
            now = parents[k, :, 0].reshape(states, nodes)
            prev = parents[k, :, 1].reshape(states, nodes)
            mixed = jnp.dot(mix[...], now, preferred_element_type=F32)
            value = (prev.astype(F32) + mixed).astype(BF16)
            for j in range(2):
                out[k, j] = lax.dot_general(
                    value, matrices[k, j], (((1,), (1,)), ((), ())), preferred_element_type=F32
                ).astype(BF16)

        @pl.when(jnp.logical_not(filled[k]))
        def _(k=k):
            out[k] = jnp.zeros(out.shape[1:], BF16)

        stores.append(
            pltpu.make_async_copy(
                out.at[k], predicted.at[pl.ds(e * 4 + rank * 2, 2)], out_sem.at[k]
            )
        )
        stores[-1].start()
    for store in stores:
        store.wait()


def predict(old, at, owners, octants, slots, pieces, tiles, interp):
    nodes = interp.shape[2]
    units = slots[0].shape[1]
    states = units * UNIT * RING * CORES
    return pl.pallas_call(
        functools.partial(predict_kernel, old),
        out_shape=sized((8, states, nodes)),
        in_specs=[SMEM] * 3 + [HBM] * 21,
        out_specs=HBM,
        scratch_shapes=[
            pltpu.VMEM((4, states // UNIT, 2, UNIT, nodes), BF16),
            pltpu.VMEM((4, 2, nodes, nodes), BF16),
            pltpu.VMEM((RING, CORES, RING, RING, 16, 128), BF16),
            pltpu.VMEM((states, states), BF16),
            pltpu.VMEM((4, 2, states, nodes), BF16),
            pltpu.SemaphoreType.DMA((4, 8)),
            pltpu.SemaphoreType.DMA((4, 2)),
            pltpu.SemaphoreType.DMA((2, RING)),
            pltpu.SemaphoreType.DMA((4,)),
        ],
        compiler_params=WHOLE_VMEM,
        cost_estimate=moved(9 << 20, 4 << 20, 24 * states * nodes * nodes),
        name="predict",
    )(at, owners, octants, slots[0], *pieces[0], slots[1], *pieces[1], *tiles, interp)


def refined(orbitals_now, orbitals_prev, interp, owner_map, child_oct):
    old, rows, nodes = orbitals_now.shape
    states = rows * lax.axis_size(BAND)
    at = jnp.stack([lax.axis_index(a) for a in DOM_BAND]).astype(jnp.int32)
    octants = child_oct.reshape(-1)
    scaling = 1.0 / math.sqrt(2.0 * states * owner_map.shape[0] * nodes)

    units = rows // UNIT
    by_unit = [a.reshape(old, units, UNIT, nodes) for a in (orbitals_now, orbitals_prev)]
    parts = (((0, 0, units),), ((1, 0, units),))
    slots, pieces = [], []
    for n in range(2):
        table = octants if n else owner_map
        slots.append(slots_for_owners(parts[n], owner_map, table, *by_unit))
        slots[n] = lax.all_to_all(slots[n], DOM, 0, 0, tiled=True)
        pieces.append(routed(at, slots[n]))
        pieces[n] = over_band(pieces[n])

    cells = cells_for_band(at, orbitals_now, orbitals_prev)
    cells = over_band(cells)
    mine, other = product_of_cells(at, octants, orbitals_now, orbitals_prev, cells, interp)
    tiles = summed_over_all(mine, other, scaling)

    return predict(old, at, owner_map, octants, slots, pieces, tiles, interp)


def solution(mesh):
    split = Mesh(mesh.devices.reshape(4, 4, 4, 2), DOM_BAND)
    placed = (P(DOM, BAND, None), P(DOM, BAND, None), P(), P(), P())
    return jax.shard_map(
        refined, mesh=split, in_specs=placed, out_specs=P(DOM_BAND, None, None), check_vma=False
    )
```

```python
import functools
import math

import jax
import jax.numpy as jnp
from jax import lax
from jax.experimental import pallas as pl
from jax.experimental.pallas import tpu as pltpu
from jax.sharding import Mesh
from jax.sharding import PartitionSpec as P


Z, X, Y, C = "dom_0", "dom_1", "band_0", "band_1"
DOM = (Z, X)
BAND = (Y, C)
DOM_BAND = (Z, X, Y, C)
CHIPS = (Z, X, Y)

BF16 = jnp.bfloat16
F32 = jnp.float32
RING = 4
CORES = 2
UNIT = 16
OFFSETS = ((0, 0), (1, 1), (3, 1), (2, 1), (1, 0), (3, 0), (2, 0), (0, 1))


WHOLE_VMEM = pltpu.CompilerParams(vmem_limit_bytes=67_043_328)

SMEM = pl.BlockSpec(memory_space=pltpu.SMEM)
HBM = pl.BlockSpec(memory_space=pltpu.HBM)


def band_pairs(q, l):
    return [
        (y * CORES + c, ((y + q) % RING) * CORES + (c + l) % CORES)
        for y in range(RING)
        for c in range(CORES)
    ]


def over_band(pieces):
    return [
        lax.ppermute(piece, BAND, band_pairs(q, l)) for (q, l), piece in zip(OFFSETS[1:], pieces)
    ]


def sized(shape, dtype=BF16):
    return jax.ShapeDtypeStruct(shape, dtype)


def moved(read, written, flops=0):
    return pl.CostEstimate(flops=flops, bytes_accessed=read + written, transcendentals=0)


def cells_kernel(at, now, prev, *refs):
    outs, (buf, in_sem, out_sem) = refs[:7], refs[7:]
    y, c = at[2], at[3]
    loads, stores = [], []
    for n, (q, l) in enumerate(OFFSETS[1:]):
        first = (((y + q) & 3) * CORES + ((c + l) & 1)) * 2
        loads.append(
            [
                pltpu.make_async_copy(src.at[pl.ds(first, 2)], buf.at[n, a], in_sem.at[n, a])
                for a, src in enumerate((now, prev))
            ]
        )
        stores.append(pltpu.make_async_copy(buf.at[n], outs[n], out_sem.at[n]))
    for pair in loads:
        for copy in pair:
            copy.start()
    for pair, store in zip(loads, stores):
        for copy in pair:
            copy.wait()
        store.start()
    for store in stores:
        store.wait()


def cells_for_band(at, now, prev):
    _, rows, nodes = now.shape
    piece = (2, 2, rows, nodes)
    size = 4 * rows * nodes * 2
    return pl.pallas_call(
        cells_kernel,
        out_shape=[sized(piece)] * 7,
        in_specs=[SMEM, HBM, HBM],
        out_specs=[HBM] * 7,
        scratch_shapes=[
            pltpu.VMEM((7, *piece), BF16),
            pltpu.SemaphoreType.DMA((7, 2)),
            pltpu.SemaphoreType.DMA((7,)),
        ],
        compiler_params=WHOLE_VMEM,
        cost_estimate=moved(7 * size, 7 * size),
        name="cells_for_band",
    )(at, now, prev)


def product_kernel(at, octants, now, prev, *refs):
    pieces, interp, mine, other = refs[:7], refs[7], refs[8], refs[9]
    parents, matrices, kids, out, in_sem, mat_sem, out_sem = refs[10:]
    z, x, y, c = at[0], at[1], at[2], at[3]
    rows = now.shape[1]
    nodes = now.shape[2]
    states = parents.shape[2]
    half = states // 2
    first = (y * CORES + c) * 2
    cell0 = (z * RING + x) * now.shape[0] + first
    loads = []
    for e in range(2):
        copies = []
        for a, src in enumerate((now, prev)):
            own = pl.ds(pl.multiple_of((y * CORES + c) * rows, rows), rows)
            copies.append(
                pltpu.make_async_copy(
                    src.at[first + e], parents.at[a, e, own], in_sem.at[e, 7 + a]
                )
            )
        for n, (q, l) in enumerate(OFFSETS[1:]):
            b = ((y - q) & 3) * CORES + ((c - l) & 1)
            to = pl.ds(pl.multiple_of(b * rows, rows), rows)
            copies.append(
                pltpu.make_async_copy(
                    pieces[n].at[:, e], parents.at[:, e, to], in_sem.at[e, n]
                )
            )
        for j in range(2):
            o = octants[(cell0 + e) * 2 + j]
            copies.append(
                pltpu.make_async_copy(interp.at[o], matrices.at[e, j], mat_sem.at[e, j])
            )
        for copy in copies:
            copy.start()
        loads.append(copies)
    for e in range(2):
        for copy in loads[e]:
            copy.wait()
        for a in range(2):
            for j in range(2):
                kids[a, :, pl.ds((e * 2 + j) * nodes, nodes)] = lax.dot_general(
                    parents[a, e],
                    matrices[e, j],
                    (((1,), (1,)), ((), ())),
                    preferred_element_type=F32,
                ).astype(BF16)
    stores = []
    for n, side in enumerate((1 - c, c)):
        u = pl.ds(pl.multiple_of(side * half, half), half)
        part = lax.dot_general(
            kids[1, u, :], kids[0], (((1,), (1,)), ((), ())), preferred_element_type=F32
        )
        for t in range(states // 128):
            out[n, t] = part[:, t * 128 : (t + 1) * 128]
        stores.append(pltpu.make_async_copy(out.at[n], mine if n else other, out_sem.at[n]))
        stores[-1].start()
    for store in stores:
        store.wait()


def product_of_cells(at, octants, now, prev, pieces, interp):
    _, rows, nodes = now.shape
    states = rows * RING * CORES
    lanes = (states // 128, states // 2, 128)
    return pl.pallas_call(
        product_kernel,
        out_shape=[sized(lanes, F32)] * 2,
        in_specs=[SMEM, SMEM] + [HBM] * 10,
        out_specs=[HBM] * 2,
        scratch_shapes=[
            pltpu.VMEM((2, 2, states, nodes), BF16),
            pltpu.VMEM((2, 2, nodes, nodes), BF16),
            pltpu.VMEM((2, states, 4 * nodes), BF16),
            pltpu.VMEM((2, *lanes), F32),
            pltpu.SemaphoreType.DMA((2, 9)),
            pltpu.SemaphoreType.DMA((2, 2)),
            pltpu.SemaphoreType.DMA((2,)),
        ],
        compiler_params=WHOLE_VMEM,
        cost_estimate=moved(4 << 20, 1 << 20, 24 * states * nodes * nodes),
        name="product_of_cells",
    )(at, octants, now, prev, *pieces, interp)


def summed_over_all(mine, other, scaling):
    swap = [(0, 1), (1, 0)]
    half = mine + lax.ppermute(other, C, swap)
    chips = lax.axis_size(CHIPS)
    tiles = lax.all_to_all(half.reshape(chips, -1, 128), CHIPS, 0, 0, tiled=True)
    own = (jnp.sum(tiles, axis=0) * scaling).astype(BF16)
    own = jnp.stack([own, lax.ppermute(own, C, swap)])
    own = jnp.broadcast_to(own[None], (chips // RING, *own.shape))
    own = lax.all_to_all(own, DOM, 0, 0, tiled=True)
    own = own.reshape(RING, RING, *own.shape[1:])
    return [own] + [
        lax.ppermute(own, Y, [(i, (i + k) % RING) for i in range(RING)])
        for k in range(1, RING)
    ]


def slots_kernel(parts, owners, octants, now, prev, out, cells, slot, seen, in_sem, out_sem):
    z, x = lax.axis_index(Z), lax.axis_index(X)
    old = now.shape[0]
    doms = RING * RING
    first = (z * RING + x) * old
    loads = [
        pltpu.make_async_copy(src, cells.at[a], in_sem.at[a]) for a, src in enumerate((now, prev))
    ]
    for load in loads:
        load.start()
    for d in range(doms):
        seen[d] = 0
        for rank in range(2):
            slot[rank * doms + d] = 0

    def place(i, carry):
        owner = owners[first + i]
        rank = jnp.minimum(seen[owner], 1)
        slot[rank * doms + owner] = i
        seen[owner] = rank + 1
        return carry

    lax.fori_loop(0, old, place, 0)
    stores = []
    for a in range(2):
        loads[a].wait()
        at_unit = 0
        for n, (rank, begin, units) in enumerate(parts):
            for d in range(doms):
                stores.append(
                    pltpu.make_async_copy(
                        cells.at[a, slot[rank * doms + d], pl.ds(begin, units)],
                        out.at[d % RING, d // RING, pl.ds(at_unit, units), a],
                        out_sem.at[n, a, d],
                    )
                )
                stores[-1].start()
            at_unit += units
    for store in stores:
        store.wait()


def slots_for_owners(parts, owners, octants, now, prev):
    old, units, _, nodes = now.shape
    doms = RING * RING
    total = sum(n for _, _, n in parts)
    size = 2 * doms * total * UNIT * nodes * 2
    return pl.pallas_call(
        functools.partial(slots_kernel, parts),
        out_shape=sized((RING, RING, total, 2, UNIT, nodes)),
        in_specs=[SMEM, SMEM, HBM, HBM],
        out_specs=HBM,
        scratch_shapes=[
            pltpu.VMEM((2, old, units, UNIT, nodes), BF16),
            pltpu.SMEM((2 * doms,), jnp.int32),
            pltpu.SMEM((doms,), jnp.int32),
            pltpu.SemaphoreType.DMA((2,)),
            pltpu.SemaphoreType.DMA((len(parts), 2, doms)),
        ],
        compiler_params=WHOLE_VMEM,
        cost_estimate=moved(size, size),
    )(owners, octants, now, prev)


def route_kernel(at, slots, *refs):
    outs, (buf, in_sem, out_sem) = refs[:7], refs[7:]
    y, c = at[2], at[3]
    loads, stores = [], []
    for n, (q, l) in enumerate(OFFSETS[1:]):
        src = slots.at[pl.ds(((c + l) & 1) * 2, 2), (y + q) & 3]
        loads.append(pltpu.make_async_copy(src, buf.at[n], in_sem.at[n]))
        stores.append(pltpu.make_async_copy(buf.at[n], outs[n], out_sem.at[n]))
    for load in loads:
        load.start()
    for load, store in zip(loads, stores):
        load.wait()
        store.start()
    for store in stores:
        store.wait()


def routed(at, slots):
    piece = (2, *slots.shape[2:])
    size = 7 * math.prod(piece) * 2
    return pl.pallas_call(
        route_kernel,
        out_shape=[sized(piece)] * 7,
        in_specs=[SMEM, HBM],
        out_specs=[HBM] * 7,
        scratch_shapes=[
            pltpu.VMEM((7, *piece), BF16),
            pltpu.SemaphoreType.DMA((7,)),
            pltpu.SemaphoreType.DMA((7,)),
        ],
        compiler_params=WHOLE_VMEM,
        cost_estimate=moved(size, size),
    )(at, slots)


def predict_kernel(old, at, owners, octants, *refs):
    slots, pieces = (refs[0], refs[8]), (refs[1:8], refs[9:16])
    tiles, interp, predicted = refs[16:20], refs[20], refs[21]
    parents, matrices, planes, mix, out, in_sem, mat_sem, mix_sem, out_sem = refs[22:]
    z, x, y, c = at[0], at[1], at[2], at[3]
    units = parents.shape[1] // (RING * CORES)
    nodes = parents.shape[4]
    states = parents.shape[1] * UNIT
    owner = z * RING + x
    mixing = []
    for n, side in enumerate((c, 1 - c)):
        for k in range(RING):
            to = planes.at[:, side, :, (y - k) & 3]
            mixing.append(pltpu.make_async_copy(tiles[k].at[:, :, n], to, mix_sem.at[n, k]))
    for copy in mixing:
        copy.start()
    loads, filled = [], []
    for k in range(4):
        rank, e = k // 2, k % 2
        first = (RING * y + 2 * c + e) * old

        def look(i, carry, first=first, rank=rank):
            count, cell = carry
            match = owners[first + i] == owner
            cell = jnp.where(match & (count == rank), i, cell)
            return count + match.astype(jnp.int32), cell

        count, cell = lax.fori_loop(0, old, look, (jnp.int32(0), jnp.int32(0)))
        filled.append(count > rank)
        copies = []
        for n, (q, l) in enumerate(OFFSETS):
            b = ((y - q) & 3) * CORES + ((c - l) & 1)
            src = pieces[rank][n - 1].at[e] if n else slots[rank].at[c * 2 + e, y]
            to = parents.at[k, pl.ds(b * units, units)]
            copies.append(pltpu.make_async_copy(src, to, in_sem.at[k, n]))
        for j in range(2):
            o = octants[(first + cell) * 2 + j]
            copies.append(
                pltpu.make_async_copy(interp.at[o], matrices.at[k, j], mat_sem.at[k, j])
            )
        for copy in copies:
            copy.start()
        loads.append(copies)
    for copy in mixing:
        copy.wait()
    for t in range(RING):
        mix[:, pl.ds(t * 128, 128)] = planes[t].reshape(states, 128)
    stores = []
    for k in range(4):
        rank, e = k // 2, k % 2
        for copy in loads[k]:
            copy.wait()

        @pl.when(filled[k])
        def _(k=k):
            now = parents[k, :, 0].reshape(states, nodes)
            prev = parents[k, :, 1].reshape(states, nodes)
            mixed = jnp.dot(mix[...], now, preferred_element_type=F32)
            value = (prev.astype(F32) + mixed).astype(BF16)
            for j in range(2):
                out[k, j] = lax.dot_general(
                    value, matrices[k, j], (((1,), (1,)), ((), ())), preferred_element_type=F32
                ).astype(BF16)

        @pl.when(jnp.logical_not(filled[k]))
        def _(k=k):
            out[k] = jnp.zeros(out.shape[1:], BF16)

        stores.append(
            pltpu.make_async_copy(
                out.at[k], predicted.at[pl.ds(e * 4 + rank * 2, 2)], out_sem.at[k]
            )
        )
        stores[-1].start()
    for store in stores:
        store.wait()


def predict(old, at, owners, octants, slots, pieces, tiles, interp):
    nodes = interp.shape[2]
    units = slots[0].shape[2]
    states = units * UNIT * RING * CORES
    return pl.pallas_call(
        functools.partial(predict_kernel, old),
        out_shape=sized((8, states, nodes)),
        in_specs=[SMEM] * 3 + [HBM] * 21,
        out_specs=HBM,
        scratch_shapes=[
            pltpu.VMEM((4, states // UNIT, 2, UNIT, nodes), BF16),
            pltpu.VMEM((4, 2, nodes, nodes), BF16),
            pltpu.VMEM((RING, CORES, RING, RING, 16, 128), BF16),
            pltpu.VMEM((states, states), BF16),
            pltpu.VMEM((4, 2, states, nodes), BF16),
            pltpu.SemaphoreType.DMA((4, 8)),
            pltpu.SemaphoreType.DMA((4, 2)),
            pltpu.SemaphoreType.DMA((2, RING)),
            pltpu.SemaphoreType.DMA((4,)),
        ],
        compiler_params=WHOLE_VMEM,
        cost_estimate=moved(9 << 20, 4 << 20, 24 * states * nodes * nodes),
        name="predict",
    )(at, owners, octants, slots[0], *pieces[0], slots[1], *pieces[1], *tiles, interp)


def refined(orbitals_now, orbitals_prev, interp, owner_map, child_oct):
    old, rows, nodes = orbitals_now.shape
    states = rows * lax.axis_size(BAND)
    at = jnp.stack([lax.axis_index(a) for a in DOM_BAND]).astype(jnp.int32)
    octants = child_oct.reshape(-1)
    scaling = 1.0 / math.sqrt(2.0 * states * owner_map.shape[0] * nodes)

    units = rows // UNIT
    by_unit = [a.reshape(old, units, UNIT, nodes) for a in (orbitals_now, orbitals_prev)]
    parts = (((0, 0, units),), ((1, 0, units),))
    slots, pieces = [], []
    for n in range(2):
        table = octants if n else owner_map
        slots.append(slots_for_owners(parts[n], owner_map, table, *by_unit))
        by_owner = slots[n].reshape(RING * RING, *slots[n].shape[2:])
        by_owner = lax.all_to_all(by_owner, (X, Z), 0, 0, tiled=True)
        slots[n] = by_owner.reshape(slots[n].shape)
        pieces.append(routed(at, slots[n]))
        pieces[n] = over_band(pieces[n])

    cells = cells_for_band(at, orbitals_now, orbitals_prev)
    cells = over_band(cells)
    mine, other = product_of_cells(at, octants, orbitals_now, orbitals_prev, cells, interp)
    tiles = summed_over_all(mine, other, scaling)

    return predict(old, at, owner_map, octants, slots, pieces, tiles, interp)


def solution(mesh):
    split = Mesh(mesh.devices.reshape(4, 4, 4, 2), DOM_BAND)
    placed = (P(DOM, BAND, None), P(DOM, BAND, None), P(), P(), P())
    return jax.shard_map(
        refined, mesh=split, in_specs=placed, out_specs=P(DOM_BAND, None, None), check_vma=False
    )
```
